32 devices in a mesh: rows: 8 (over z, x), cols: 4 (over y, core).
Axes of the slice: x: 2, y: 2, z: 4, core: 2. Of those that a mesh axis runs over, the one named last changes fastest.
Arguments:
- panel_cols: float32 [65536, 256], P(('rows', 'cols')), may hold values from -10000 to 10000, as said below
- trailing: float32 [65536, 1024], P('rows', 'cols'), may hold values from -200000 to 200000
Outputs:
- r_factor: float32 [256, 256], replicated
- r_cross: float32 [256, 1024], P(None, 'cols')
- updated: float32 [65536, 1024], P('rows', 'cols')
The draws below stay inside these ranges and needn't reach their ends.
Inputs may be any that keep to these rules, and one draw needn't show every extreme that they name: panel_cols has full column rank.
All inputs are finite; a program needn't handle non-finite values.
Results may differ from the reference program's by a relative error of at most 0.0003.
Values sent between devices are 32-bit elements; how exact they have to be, the bound alone decides.
A program may use at most 128 MiB of HBM per device.

```python
import math
import jax
import jax.numpy as jnp
from jax import lax

B = 256
NC = 1024
ROWS = 65536


def panel_matrix(key):
    keys = jax.random.split(jax.random.fold_in(key, 11), 4)
    position = jnp.arange(ROWS, dtype=jnp.float32) / ROWS
    base_entries = jnp.clip(jax.random.normal(keys[0], (ROWS, B), jnp.float32), -6.0, 6.0)
    spread = jax.random.uniform(keys[1], (ROWS, 1), jnp.float32, 0.0, 1.0)
    row_scale = jnp.power(10.0, spread) * jnp.power(3.0, 0.5 * position)[:, None] / 6.0
    column_scale = jnp.exp(jax.random.uniform(keys[2], (B,), jnp.float32, 0.0, math.log(10.0)))
    perturb = jnp.clip(jax.random.normal(keys[3], (B, B), jnp.float32), -6.0, 6.0) * (0.35 / math.sqrt(B))
    mixing = (jnp.eye(B, dtype=jnp.float32) + perturb) * column_scale[None, :]
    return jnp.dot(base_entries * row_scale, mixing, precision=lax.Precision.HIGHEST)


def draw_panel_cols(key, part):
    return panel_matrix(key)


def draw_trailing(key, part):
    matrix = panel_matrix(key)
    keys = jax.random.split(jax.random.fold_in(key, 23), 2)
    coeffs = jnp.clip(jax.random.normal(keys[0], (B, NC), jnp.float32), -6.0, 6.0) * (0.6 / (4.6 * math.sqrt(B)))
    noise = jnp.clip(jax.random.normal(keys[1], (ROWS, NC), jnp.float32), -6.0, 6.0)
    return jnp.dot(matrix, coeffs, precision=lax.Precision.HIGHEST) + noise


def setup_inputs(seed: int = 0) -> dict:
    splits = jax.random.split(jax.random.key(seed), 3)
    return {
        "panel_cols": draw_panel_cols(jax.random.fold_in(splits[2], 71), 0),
        "trailing": draw_trailing(jax.random.fold_in(splits[2], 71), 0),
    }


def reference(panel_cols, trailing):
    orthonormal, upper_factor = jnp.linalg.qr(panel_cols, mode='reduced')
    sign_flip = jnp.where(jnp.diagonal(upper_factor) < 0, -1.0, 1.0).astype(upper_factor.dtype)
    upper_factor = upper_factor * sign_flip[:, None]
    orthonormal = orthonormal * sign_flip[None, :]
    coupling = jnp.dot(orthonormal.T, trailing, precision=lax.Precision.HIGHEST)
    updated = trailing - jnp.dot(orthonormal, coupling, precision=lax.Precision.HIGHEST)
    shrink = 1.0 / math.sqrt(ROWS)
    return (upper_factor * shrink, coupling * shrink, updated)
```

```python
import functools
import math

import jax
import jax.numpy as jnp
from jax import lax
from jax.experimental import pallas as pl
from jax.experimental.pallas import tpu as pltpu

MESH = pl.DeviceIdType.MESH
HIGHEST = lax.Precision.HIGHEST
CHUNKS = 8
EARLY = 3
GROUP = 4


def dot(left, right):
    return lax.dot_general(left, right, (((1,), (0,)), ((), ())), precision=HIGHEST, preferred_element_type=jnp.float32)


def dot_t(left, right):
    return lax.dot_general(left, right, (((0,), (0,)), ((), ())), precision=HIGHEST, preferred_element_type=jnp.float32)


def eliminate(a_ref, m_ref, first, last):
    size = a_ref.shape[0]
    sub = lax.broadcasted_iota(jnp.int32, (size, 1), 0)
    lane = lax.broadcasted_iota(jnp.int32, (size, size), 1)
    lane_row = lax.broadcasted_iota(jnp.int32, (1, size), 1)

    def step(index, carry):
        j = index * GROUP
        a = a_ref[...]
        rows = [a_ref[pl.ds(j + t, 1), :] for t in range(GROUP)]
        mrows = [m_ref[pl.ds(j + t, 1), :] for t in range(GROUP)]
        cols = [jnp.sum(jnp.where(lane == j + t, a, 0.0), axis=1, keepdims=True) for t in range(GROUP)]
        head = {
            (t, u): jnp.sum(jnp.where(lane_row == j + u, rows[t], 0.0), axis=1, keepdims=True)
            for t in range(GROUP)
            for u in range(t, GROUP)
        }
        m = m_ref[...]
        for t in range(GROUP):
            inverse = 1.0 / head[t, t]
            factor = jnp.where(sub > j + t, cols[t] * inverse, 0.0)
            ratio = {u: head[t, u] * inverse for u in range(t + 1, GROUP)}
            for u in range(t + 1, GROUP):
                cols[u] = cols[u] - factor * head[t, u]
            for u in range(t + 1, GROUP):
                for v in range(u, GROUP):
                    head[u, v] = head[u, v] - ratio[u] * head[t, v]
            for u in range(t + 1, GROUP):
                rows[u] = rows[u] - ratio[u] * rows[t]
                mrows[u] = mrows[u] - ratio[u] * mrows[t]
            a = a - factor * rows[t]
            m = m - factor * mrows[t]
        a_ref[...] = a
        m_ref[...] = m
        return carry

    lax.fori_loop(first // GROUP, last // GROUP, step, 0)


def scale_rows(a_ref, m_ref):
    size = a_ref.shape[0]
    sub = lax.broadcasted_iota(jnp.int32, (size, size), 0)
    lane = lax.broadcasted_iota(jnp.int32, (size, size), 1)
    a = a_ref[...]
    diagonal = jnp.sum(jnp.where(lane == sub, a, 0.0), axis=1, keepdims=True)
    scale = 1.0 / jnp.sqrt(diagonal)
    return jnp.where(lane >= sub, a * scale, 0.0), m_ref[...] * scale


def unit(size):
    sub = lax.broadcasted_iota(jnp.int32, (size, size), 0)
    lane = lax.broadcasted_iota(jnp.int32, (size, size), 1)
    return jnp.where(lane == sub, 1.0, 0.0).astype(jnp.float32)


def factor_kernel(
    nr, nc,
    panel, trailing, block_out, upper_out, coupling_out, weights_out,
    block, trail, gram, gram_stage, col_stage, gram_sum, cross, cross_stage, cross_sum, work, minv,
    load_sem, out_sem, y_send, y_recv, half_send, half_recv, fwd_send, fwd_recv,
    rs_send, rs_recv, cx_send, cx_recv, ag_send, ag_recv, xrs_send, xrs_recv, xag_send, xag_recv,
):
    me_r, me_c = lax.axis_index("rows"), lax.axis_index("cols")
    depth, width = panel.shape
    half = nc // 2
    side, place = me_c // half, lax.rem(me_c, half)
    across = lax.rem(me_c + half, nc)
    chunk = depth // CHUNKS
    piece = width // nr
    hw = width // 2
    sends = []

    def remote(src, dst, send, recv, where):
        copy = pltpu.make_async_remote_copy(
            src_ref=src, dst_ref=dst, send_sem=send, recv_sem=recv, device_id=where, device_id_type=MESH
        )
        copy.start()
        sends.append(copy)
        return copy

    load_panel = pltpu.make_async_copy(panel, block.at[me_c], load_sem.at[0])
    load_panel.start()
    load_trail = pltpu.make_async_copy(trailing, trail, load_sem.at[1])
    load_trail.start()

    barrier = pltpu.get_barrier_semaphore()
    for d in range(1, nr):
        pl.semaphore_signal(barrier, inc=1, device_id={"rows": lax.rem(me_r + d, nr)}, device_id_type=MESH)
    for d in range(1, nc):
        pl.semaphore_signal(barrier, inc=1, device_id={"cols": lax.rem(me_c + d, nc)}, device_id_type=MESH)
    pl.semaphore_wait(barrier, nr + nc - 2)

    y_copies = []

    def send_across(k):
        rows = pl.ds(k * chunk, chunk)
        y_copies.append(
            remote(panel.at[rows], block.at[me_c, rows], y_send.at[k], y_recv.at[k], {"cols": across})
        )

    for k in range(EARLY):
        send_across(k)
    half_copies = []
    for d in range(1, half):
        peer = side * half + lax.rem(place + d, half)
        half_copies.append(remote(panel, block.at[me_c], half_send.at[d], half_recv.at[d], {"cols": peer}))

    def add_cross(source, first, count):
        def step(i, carry):
            rows = pl.ds(pl.multiple_of(i * chunk, chunk), chunk)
            wide = pl.ds(pl.multiple_of(source * depth + i * chunk, chunk), chunk)
            cross[...] += dot_t(block[source, rows, :], trail[wide, :])
            return carry

        lax.fori_loop(first, first + count, step, 0)

    def store_block(source, first, count, slot):
        rows = pl.ds(first * chunk, count * chunk)
        wide = pl.ds(pl.multiple_of(source * depth + first * chunk, chunk), count * chunk)
        copy = pltpu.make_async_copy(block.at[source, rows], block_out.at[wide], out_sem.at[slot])
        copy.start()
        outs.append(copy)

    outs = []

    load_panel.wait()
    gram[...] = jnp.zeros_like(gram)

    def gram_step(i, carry):
        rows = block[me_c, pl.ds(pl.multiple_of(i * chunk, chunk), chunk), :]
        gram[...] += dot_t(rows, rows)
        return carry

    lax.fori_loop(0, CHUNKS, gram_step, 0)

    def scatter(total, stage, send, recv):
        copies = []
        for d in range(1, nr):
            peer = lax.rem(me_r + d, nr)
            rows = pl.ds(pl.multiple_of(peer * piece, piece), piece)
            copies.append(remote(total.at[rows], stage.at[d], send.at[d], recv.at[d], {"rows": peer}))
        return copies

    def gather(total, send, recv):
        rows = pl.ds(pl.multiple_of(me_r * piece, piece), piece)
        return [
            remote(total.at[rows], total.at[rows], send.at[d], recv.at[d], {"rows": lax.rem(me_r + d, nr)})
            for d in range(1, nr)
        ]

    def arrived(copies):
        for copy in copies:
            copy.wait_recv()

    mine = pl.ds(pl.multiple_of(me_r * piece, piece), piece)

    def summed(total, stage):
        value = total[mine, :]
        for d in range(1, nr):
            value = value + stage[d]
        return value

    gram_rs = scatter(gram, gram_stage, rs_send, rs_recv)
    load_trail.wait()
    cross[...] = jnp.zeros_like(cross)
    add_cross(me_c, 0, CHUNKS)
    store_block(me_c, 0, CHUNKS, 0)
    arrived(gram_rs)
    col_stage[me_c] = summed(gram, gram_stage)
    exchange = [
        remote(col_stage.at[me_c], col_stage.at[me_c], cx_send.at[d], cx_recv.at[d], {"cols": lax.rem(me_c + d, nc)})
        for d in range(1, nc)
    ]
    for k in range(EARLY, CHUNKS):
        send_across(k)
    for d in range(1, half):
        half_copies[d - 1].wait_recv()
        source = side * half + lax.rem(place + half - d, half)
        store_block(source, 0, CHUNKS, d)
        add_cross(source, 0, CHUNKS)
    arrived(exchange)
    value = col_stage[0]
    for c in range(1, nc):
        value = value + col_stage[c]
    gram_sum[mine, :] = value
    gram_ag = gather(gram_sum, ag_send, ag_recv)

    forwards = {}

    def take(k):
        y_copies[k].wait_recv()
        rows = pl.ds(k * chunk, chunk)
        for d in range(1, half):
            peer = side * half + lax.rem(place + d, half)
            slot = (d - 1) * CHUNKS + k
            forwards[d, k] = remote(
                block.at[across, rows], block.at[across, rows], fwd_send.at[slot], fwd_recv.at[slot], {"cols": peer}
            )
        add_cross(across, k, 1)
        store_block(across, k, 1, half + k)

    def take_forward(k):
        for d in range(1, half):
            forwards[d, k].wait_recv()
            source = (1 - side) * half + lax.rem(place + half - d, half)
            add_cross(source, k, 1)
            store_block(source, k, 1, half + CHUNKS * d + k)

    for k in range(EARLY):
        take(k)
        if k:
            take_forward(k - 1)

    def run(first, last, k):
        eliminate(work, minv, first, last)
        if k is not None:
            take(k)
            take_forward(k - 1)

    arrived(gram_ag)
    work[...] = gram_sum[pl.ds(0, hw), pl.ds(0, hw)]
    minv[...] = unit(hw)
    quarter = hw // 4
    run(0, quarter, EARLY)
    run(quarter, 2 * quarter, None)
    run(2 * quarter, 3 * quarter, EARLY + 1)
    run(3 * quarter, hw, None)
    upper1, inverse1 = scale_rows(work, minv)
    cross1 = dot(inverse1, gram_sum[pl.ds(0, hw), pl.ds(hw, hw)])
    upper_out[pl.ds(0, hw), pl.ds(0, hw)] = upper1
    upper_out[pl.ds(0, hw), pl.ds(hw, hw)] = cross1
    upper_out[pl.ds(hw, hw), pl.ds(0, hw)] = jnp.zeros_like(upper1)
    work[...] = gram_sum[pl.ds(hw, hw), pl.ds(hw, hw)] - dot_t(cross1, cross1)
    weights_out[pl.ds(0, hw), pl.ds(0, hw)] = inverse1
    minv[...] = unit(hw)
    run(0, quarter, EARLY + 2)
    run(quarter, 2 * quarter, EARLY + 3)
    run(2 * quarter, 3 * quarter, EARLY + 4)
    take_forward(CHUNKS - 1)
    cross_rs = scatter(cross, cross_stage, xrs_send, xrs_recv)
    run(3 * quarter, hw, None)
    upper2, inverse2 = scale_rows(work, minv)
    upper_out[pl.ds(hw, hw), pl.ds(hw, hw)] = upper2
    inverse1 = weights_out[pl.ds(0, hw), pl.ds(0, hw)]
    corner = -dot(inverse2, dot_t(upper_out[pl.ds(0, hw), pl.ds(hw, hw)], inverse1))
    weights_out[pl.ds(0, hw), pl.ds(hw, hw)] = jnp.zeros_like(inverse1)
    weights_out[pl.ds(hw, hw), pl.ds(0, hw)] = corner
    weights_out[pl.ds(hw, hw), pl.ds(hw, hw)] = inverse2
    arrived(cross_rs)
    cross_sum[mine, :] = summed(cross, cross_stage)
    cross_ag = gather(cross_sum, xag_send, xag_recv)
    for copy in outs:
        copy.wait()
    arrived(cross_ag)
    inverse = weights_out[...]
    coupling = dot(inverse, cross_sum[...])
    coupling_out[...] = coupling
    weights_out[...] = dot_t(inverse, coupling)
    for copy in sends:
        copy.wait_send()


def update_kernel(shrink, block, trailing, upper, coupling, weights, r_factor, r_cross, updated, w_hi, w_lo):
    @pl.when(pl.program_id(0) == 0)
    def _():
        r_factor[...] = upper[...] * shrink
        r_cross[...] = coupling[...] * shrink
        w = weights[...]
        high = w.astype(jnp.bfloat16)
        w_hi[...] = high
        w_lo[...] = (w - high.astype(jnp.float32)).astype(jnp.bfloat16)

    p = block[...]
    p_hi = p.astype(jnp.bfloat16)
    p_lo = (p - p_hi.astype(jnp.float32)).astype(jnp.bfloat16)

    def mul(left, right):
        return jnp.dot(left, right, preferred_element_type=jnp.float32)

    product = mul(p_hi, w_hi[...]) + (mul(p_lo, w_hi[...]) + mul(p_hi, w_lo[...]))
    updated[...] = trailing[...] - product


def local(nr, nc, panel_cols, trailing):
    depth, width = panel_cols.shape
    rows, cols = trailing.shape
    half = nc // 2
    piece = width // nr
    f32 = jnp.float32
    square = jax.ShapeDtypeStruct((width, width), f32)
    tall = jax.ShapeDtypeStruct((width, cols), f32)
    dma = pltpu.SemaphoreType.DMA
    vmem = pl.BlockSpec(memory_space=pltpu.VMEM)
    hbm = pl.BlockSpec(memory_space=pl.ANY)
    block, upper, coupling, weights = pl.pallas_call(
        functools.partial(factor_kernel, nr, nc),
        out_shape=(jax.ShapeDtypeStruct((rows, width), f32), square, tall, tall),
        in_specs=[hbm, hbm],
        out_specs=(hbm, vmem, vmem, vmem),
        scratch_shapes=[
            pltpu.VMEM((nc, depth, width), f32),
            pltpu.VMEM((rows, cols), f32),
            pltpu.VMEM((width, width), f32),
            pltpu.VMEM((nr, piece, width), f32),
            pltpu.VMEM((nc, piece, width), f32),
            pltpu.VMEM((width, width), f32),
            pltpu.VMEM((width, cols), f32),
            pltpu.VMEM((nr, piece, cols), f32),
            pltpu.VMEM((width, cols), f32),
            pltpu.VMEM((width // 2, width // 2), f32),
            pltpu.VMEM((width // 2, width // 2), f32),
            dma((2,)),
            dma((half + CHUNKS * half,)),
            dma((CHUNKS,)), dma((CHUNKS,)),
            dma((half,)), dma((half,)),
            dma((CHUNKS * half,)), dma((CHUNKS * half,)),
            dma((nr,)), dma((nr,)),
            dma((nc,)), dma((nc,)),
            dma((nr,)), dma((nr,)),
            dma((nr,)), dma((nr,)),
            dma((nr,)), dma((nr,)),
        ],
        compiler_params=pltpu.CompilerParams(
            collective_id=0, has_side_effects=True, vmem_limit_bytes=40 * 1024 * 1024
        ),
        name="factor",
    )(panel_cols, trailing)

    tile = rows // 8
    fixed = lambda i: (0, 0)
    shrink = 1.0 / math.sqrt(rows * nr)
    r_factor, r_cross, updated = pl.pallas_call(
        functools.partial(update_kernel, shrink),
        grid=(rows // tile,),
        out_shape=(square, tall, jax.ShapeDtypeStruct((rows, cols), f32)),
        in_specs=[
            pl.BlockSpec((tile, width), lambda i: (i, 0)),
            pl.BlockSpec((tile, cols), lambda i: (i, 0)),
            pl.BlockSpec((width, width), fixed),
            pl.BlockSpec((width, cols), fixed),
            pl.BlockSpec((width, cols), fixed),
        ],
        out_specs=(
            pl.BlockSpec((width, width), fixed),
            pl.BlockSpec((width, cols), fixed),
            pl.BlockSpec((tile, cols), lambda i: (i, 0)),
        ),
        scratch_shapes=[pltpu.VMEM((width, cols), jnp.bfloat16)] * 2,
        name="update",
    )(block, trailing, upper, coupling, weights)
    return r_factor, r_cross, updated


def solution(mesh):
    P = jax.sharding.PartitionSpec
    body = functools.partial(local, mesh.shape["rows"], mesh.shape["cols"])
    in_specs = (P(("rows", "cols"), None), P("rows", "cols"))
    out_specs = (P(), P(None, "cols"), P("rows", "cols"))
    return jax.shard_map(body, mesh=mesh, in_specs=in_specs, out_specs=out_specs, check_vma=False)
```

```python
import functools
import math

import jax
import jax.numpy as jnp
from jax import lax
from jax.experimental import pallas as pl
from jax.experimental.pallas import tpu as pltpu

MESH = pl.DeviceIdType.MESH
HIGHEST = lax.Precision.HIGHEST
CHUNKS = 8
EARLY = 3
GROUP = 4
TILES = 16


def dot(left, right):
    return lax.dot_general(left, right, (((1,), (0,)), ((), ())), precision=HIGHEST, preferred_element_type=jnp.float32)


def dot_t(left, right):
    return lax.dot_general(left, right, (((0,), (0,)), ((), ())), precision=HIGHEST, preferred_element_type=jnp.float32)


def eliminate(a_ref, m_ref, first, last):
    size = a_ref.shape[0]
    sub = lax.broadcasted_iota(jnp.int32, (size, 1), 0)
    lane = lax.broadcasted_iota(jnp.int32, (size, size), 1)
    lane_row = lax.broadcasted_iota(jnp.int32, (1, size), 1)

    def step(index, carry):
        j = index * GROUP
        a = a_ref[...]
        rows = [a_ref[pl.ds(j + t, 1), :] for t in range(GROUP)]
        mrows = [m_ref[pl.ds(j + t, 1), :] for t in range(GROUP)]
        cols = [jnp.sum(jnp.where(lane == j + t, a, 0.0), axis=1, keepdims=True) for t in range(GROUP)]
        head = {
            (t, u): jnp.sum(jnp.where(lane_row == j + u, rows[t], 0.0), axis=1, keepdims=True)
            for t in range(GROUP)
            for u in range(t, GROUP)
        }
        m = m_ref[...]
        for t in range(GROUP):
            inverse = 1.0 / head[t, t]
            factor = jnp.where(sub > j + t, cols[t] * inverse, 0.0)
            ratio = {u: head[t, u] * inverse for u in range(t + 1, GROUP)}
            for u in range(t + 1, GROUP):
                cols[u] = cols[u] - factor * head[t, u]
            for u in range(t + 1, GROUP):
                for v in range(u, GROUP):
                    head[u, v] = head[u, v] - ratio[u] * head[t, v]
            for u in range(t + 1, GROUP):
                rows[u] = rows[u] - ratio[u] * rows[t]
                mrows[u] = mrows[u] - ratio[u] * mrows[t]
            a = a - factor * rows[t]
            m = m - factor * mrows[t]
        a_ref[...] = a
        m_ref[...] = m
        return carry

    lax.fori_loop(first // GROUP, last // GROUP, step, 0)


def scale_rows(a_ref, m_ref):
    size = a_ref.shape[0]
    sub = lax.broadcasted_iota(jnp.int32, (size, size), 0)
    lane = lax.broadcasted_iota(jnp.int32, (size, size), 1)
    a = a_ref[...]
    diagonal = jnp.sum(jnp.where(lane == sub, a, 0.0), axis=1, keepdims=True)
    scale = 1.0 / jnp.sqrt(diagonal)
    return jnp.where(lane >= sub, a * scale, 0.0), m_ref[...] * scale


def unit(size):
    sub = lax.broadcasted_iota(jnp.int32, (size, size), 0)
    lane = lax.broadcasted_iota(jnp.int32, (size, size), 1)
    return jnp.where(lane == sub, 1.0, 0.0).astype(jnp.float32)


def factor_kernel(
    nr, nc,
    panel, trailing, block, trail, upper_out, coupling_out, weights_out,
    gram, gram_stage, col_stage, gram_sum, cross, cross_stage, cross_sum, work, minv,
    load_sem, y_send, y_recv, half_send, half_recv, fwd_send, fwd_recv,
    rs_send, rs_recv, cx_send, cx_recv, ag_send, ag_recv, xrs_send, xrs_recv, xag_send, xag_recv,
):
    me_r, me_c = lax.axis_index("rows"), lax.axis_index("cols")
    depth, width = panel.shape
    half = nc // 2
    side, place = me_c // half, lax.rem(me_c, half)
    across = lax.rem(me_c + half, nc)
    chunk = depth // CHUNKS
    piece = width // nr
    hw = width // 2
    sends = []

    def remote(src, dst, send, recv, where):
        copy = pltpu.make_async_remote_copy(
            src_ref=src, dst_ref=dst, send_sem=send, recv_sem=recv, device_id=where, device_id_type=MESH
        )
        copy.start()
        sends.append(copy)
        return copy

    load_panel = pltpu.make_async_copy(panel, block.at[me_c], load_sem.at[0])
    load_panel.start()
    load_trail = pltpu.make_async_copy(trailing, trail, load_sem.at[1])
    load_trail.start()

    barrier = pltpu.get_barrier_semaphore()
    for d in range(1, nr):
        pl.semaphore_signal(barrier, inc=1, device_id={"rows": lax.rem(me_r + d, nr)}, device_id_type=MESH)
    for d in range(1, nc):
        pl.semaphore_signal(barrier, inc=1, device_id={"cols": lax.rem(me_c + d, nc)}, device_id_type=MESH)
    pl.semaphore_wait(barrier, nr + nc - 2)

    y_copies = []

    def send_across(k):
        rows = pl.ds(k * chunk, chunk)
        y_copies.append(
            remote(panel.at[rows], block.at[me_c, rows], y_send.at[k], y_recv.at[k], {"cols": across})
        )

    for k in range(EARLY):
        send_across(k)
    half_copies = []
    for d in range(1, half):
        peer = side * half + lax.rem(place + d, half)
        half_copies.append(remote(panel, block.at[me_c], half_send.at[d], half_recv.at[d], {"cols": peer}))

    def add_cross(source, first, count):
        def step(i, carry):
            rows = pl.ds(pl.multiple_of(i * chunk, chunk), chunk)
            wide = pl.ds(pl.multiple_of(source * depth + i * chunk, chunk), chunk)
            cross[...] += dot_t(block[source, rows, :], trail[wide, :])
            return carry

        lax.fori_loop(first, first + count, step, 0)

    load_panel.wait()
    gram[...] = jnp.zeros_like(gram)

    def gram_step(i, carry):
        rows = block[me_c, pl.ds(pl.multiple_of(i * chunk, chunk), chunk), :]
        gram[...] += dot_t(rows, rows)
        return carry

    lax.fori_loop(0, CHUNKS, gram_step, 0)

    def scatter(total, stage, send, recv):
        copies = []
        for d in range(1, nr):
            peer = lax.rem(me_r + d, nr)
            rows = pl.ds(pl.multiple_of(peer * piece, piece), piece)
            copies.append(remote(total.at[rows], stage.at[d], send.at[d], recv.at[d], {"rows": peer}))
        return copies

    def gather(total, send, recv):
        rows = pl.ds(pl.multiple_of(me_r * piece, piece), piece)
        return [
            remote(total.at[rows], total.at[rows], send.at[d], recv.at[d], {"rows": lax.rem(me_r + d, nr)})
            for d in range(1, nr)
        ]

    def arrived(copies):
        for copy in copies:
            copy.wait_recv()

    mine = pl.ds(pl.multiple_of(me_r * piece, piece), piece)

    def summed(total, stage):
        value = total[mine, :]
        for d in range(1, nr):
            value = value + stage[d]
        return value

    gram_rs = scatter(gram, gram_stage, rs_send, rs_recv)
    load_trail.wait()
    cross[...] = jnp.zeros_like(cross)
    add_cross(me_c, 0, CHUNKS)
    arrived(gram_rs)
    col_stage[me_c] = summed(gram, gram_stage)
    exchange = [
        remote(col_stage.at[me_c], col_stage.at[me_c], cx_send.at[d], cx_recv.at[d], {"cols": lax.rem(me_c + d, nc)})
        for d in range(1, nc)
    ]
    for k in range(EARLY, CHUNKS):
        send_across(k)
    for d in range(1, half):
        half_copies[d - 1].wait_recv()
        source = side * half + lax.rem(place + half - d, half)
        add_cross(source, 0, CHUNKS)
    arrived(exchange)
    value = col_stage[0]
    for c in range(1, nc):
        value = value + col_stage[c]
    gram_sum[mine, :] = value
    gram_ag = gather(gram_sum, ag_send, ag_recv)

    forwards = {}

    def take(k):
        y_copies[k].wait_recv()
        rows = pl.ds(k * chunk, chunk)
        for d in range(1, half):
            peer = side * half + lax.rem(place + d, half)
            slot = (d - 1) * CHUNKS + k
            forwards[d, k] = remote(
                block.at[across, rows], block.at[across, rows], fwd_send.at[slot], fwd_recv.at[slot], {"cols": peer}
            )
        add_cross(across, k, 1)

    def take_forward(k):
        for d in range(1, half):
            forwards[d, k].wait_recv()
            source = (1 - side) * half + lax.rem(place + half - d, half)
            add_cross(source, k, 1)

    for k in range(EARLY):
        take(k)
        if k:
            take_forward(k - 1)

    def run(first, last, k):
        eliminate(work, minv, first, last)
        if k is not None:
            take(k)
            take_forward(k - 1)

    arrived(gram_ag)
    work[...] = gram_sum[pl.ds(0, hw), pl.ds(0, hw)]
    minv[...] = unit(hw)
    quarter = hw // 4
    run(0, quarter, EARLY)
    run(quarter, 2 * quarter, None)
    run(2 * quarter, 3 * quarter, EARLY + 1)
    run(3 * quarter, hw, None)
    upper1, inverse1 = scale_rows(work, minv)
    cross1 = dot(inverse1, gram_sum[pl.ds(0, hw), pl.ds(hw, hw)])
    upper_out[pl.ds(0, hw), pl.ds(0, hw)] = upper1
    upper_out[pl.ds(0, hw), pl.ds(hw, hw)] = cross1
    upper_out[pl.ds(hw, hw), pl.ds(0, hw)] = jnp.zeros_like(upper1)
    work[...] = gram_sum[pl.ds(hw, hw), pl.ds(hw, hw)] - dot_t(cross1, cross1)
    weights_out[pl.ds(0, hw), pl.ds(0, hw)] = inverse1
    minv[...] = unit(hw)
    run(0, quarter, EARLY + 2)
    run(quarter, 2 * quarter, EARLY + 3)
    run(2 * quarter, 3 * quarter, EARLY + 4)
    take_forward(CHUNKS - 1)
    cross_rs = scatter(cross, cross_stage, xrs_send, xrs_recv)
    run(3 * quarter, hw, None)
    upper2, inverse2 = scale_rows(work, minv)
    upper_out[pl.ds(hw, hw), pl.ds(hw, hw)] = upper2
    inverse1 = weights_out[pl.ds(0, hw), pl.ds(0, hw)]
    corner = -dot(inverse2, dot_t(upper_out[pl.ds(0, hw), pl.ds(hw, hw)], inverse1))
    weights_out[pl.ds(0, hw), pl.ds(hw, hw)] = jnp.zeros_like(inverse1)
    weights_out[pl.ds(hw, hw), pl.ds(0, hw)] = corner
    weights_out[pl.ds(hw, hw), pl.ds(hw, hw)] = inverse2
    arrived(cross_rs)
    cross_sum[mine, :] = summed(cross, cross_stage)
    cross_ag = gather(cross_sum, xag_send, xag_recv)
    arrived(cross_ag)
    inverse = weights_out[...]
    coupling = dot(inverse, cross_sum[...])
    coupling_out[...] = coupling
    weights_out[...] = dot_t(inverse, coupling)
    for copy in sends:
        copy.wait_send()


def update_kernel(
    shrink, block, trailing, upper, coupling, weights, r_factor, r_cross, updated,
    small, w_hi, w_lo, out, small_sem, out_sem,
):
    small[0] = upper[...] * shrink
    small[1] = coupling[...] * shrink
    copies = [
        pltpu.make_async_copy(small.at[0], r_factor, small_sem.at[0]),
        pltpu.make_async_copy(small.at[1], r_cross, small_sem.at[1]),
    ]
    for copy in copies:
        copy.start()
    w = weights[...]
    high = w.astype(jnp.bfloat16)
    w_hi[...] = high
    w_lo[...] = (w - high.astype(jnp.float32)).astype(jnp.bfloat16)
    tile = out.shape[0] // TILES

    def mul(left, right):
        return jnp.dot(left, right, preferred_element_type=jnp.float32)

    def window(i):
        return pl.ds(pl.multiple_of(i * tile, tile), tile)

    def store(i):
        return pltpu.make_async_copy(out.at[window(i)], updated.at[window(i)], out_sem.at[i])

    def step(i, carry):
        rows = window(i)
        p = block[rows, :]
        p_hi = p.astype(jnp.bfloat16)
        p_lo = (p - p_hi.astype(jnp.float32)).astype(jnp.bfloat16)
        product = mul(p_hi, w_hi[...]) + (mul(p_lo, w_hi[...]) + mul(p_hi, w_lo[...]))
        out[rows, :] = trailing[rows, :] - product
        store(i).start()
        return carry

    lax.fori_loop(0, TILES, step, 0)
    for i in range(TILES):
        store(i).wait()
    for copy in copies:
        copy.wait()


def local(nr, nc, panel_cols, trailing):
    depth, width = panel_cols.shape
    rows, cols = trailing.shape
    half = nc // 2
    piece = width // nr
    f32 = jnp.float32
    square = jax.ShapeDtypeStruct((width, width), f32)
    tall = jax.ShapeDtypeStruct((width, cols), f32)
    dma = pltpu.SemaphoreType.DMA
    vmem = pl.BlockSpec(memory_space=pltpu.VMEM)
    hbm = pl.BlockSpec(memory_space=pltpu.HBM)
    block, trail, upper, coupling, weights = pl.pallas_call(
        functools.partial(factor_kernel, nr, nc),
        out_shape=(jax.ShapeDtypeStruct((nc, depth, width), f32), jax.ShapeDtypeStruct((rows, cols), f32), square, tall, tall),
        in_specs=[hbm, hbm],
        out_specs=(vmem,) * 5,
        scratch_shapes=[
            pltpu.VMEM((width, width), f32),
            pltpu.VMEM((nr, piece, width), f32),
            pltpu.VMEM((nc, piece, width), f32),
            pltpu.VMEM((width, width), f32),
            pltpu.VMEM((width, cols), f32),
            pltpu.VMEM((nr, piece, cols), f32),
            pltpu.VMEM((width, cols), f32),
            pltpu.VMEM((width // 2, width // 2), f32),
            pltpu.VMEM((width // 2, width // 2), f32),
            dma((2,)),
            dma((CHUNKS,)), dma((CHUNKS,)),
            dma((half,)), dma((half,)),
            dma((CHUNKS * half,)), dma((CHUNKS * half,)),
            dma((nr,)), dma((nr,)),
            dma((nc,)), dma((nc,)),
            dma((nr,)), dma((nr,)),
            dma((nr,)), dma((nr,)),
            dma((nr,)), dma((nr,)),
        ],
        compiler_params=pltpu.CompilerParams(
            collective_id=0, has_side_effects=True, vmem_limit_bytes=20 * 1024 * 1024
        ),
        name="factor",
    )(*(pltpu.with_memory_space_constraint(x, pltpu.HBM) for x in (panel_cols, trailing)))

    shrink = 1.0 / math.sqrt(rows * nr)
    r_factor, r_cross, updated = pl.pallas_call(
        functools.partial(update_kernel, shrink),
        out_shape=(square, tall, jax.ShapeDtypeStruct((rows, cols), f32)),
        in_specs=[vmem] * 5,
        out_specs=(hbm,) * 3,
        scratch_shapes=[
            pltpu.VMEM((2, width, cols), f32),
            pltpu.VMEM((width, cols), jnp.bfloat16),
            pltpu.VMEM((width, cols), jnp.bfloat16),
            pltpu.VMEM((rows, cols), f32),
            dma((2,)),
            dma((TILES,)),
        ],
        compiler_params=pltpu.CompilerParams(vmem_limit_bytes=24 * 1024 * 1024),
        name="update",
    )(block.reshape(rows, width), trail, upper, coupling, weights)
    return r_factor, r_cross, updated


def solution(mesh):
    P = jax.sharding.PartitionSpec
    body = functools.partial(local, mesh.shape["rows"], mesh.shape["cols"])
    in_specs = (P(("rows", "cols"), None), P("rows", "cols"))
    out_specs = (P(), P(None, "cols"), P("rows", "cols"))
    return jax.shard_map(body, mesh=mesh, in_specs=in_specs, out_specs=out_specs, check_vma=False)
```

```python
import functools
import math

import jax
import jax.numpy as jnp
from jax import lax
from jax.experimental import pallas as pl
from jax.experimental.pallas import tpu as pltpu

MESH = pl.DeviceIdType.MESH
HIGHEST = lax.Precision.HIGHEST
CHUNKS = 8
EARLY = 3
MORE = (1, 1, 1, 0, 1, 0, 1, 0)
GROUP = 4
TILES = 16


def dot(left, right):
    return lax.dot_general(left, right, (((1,), (0,)), ((), ())), precision=HIGHEST, preferred_element_type=jnp.float32)


def dot_t(left, right):
    return lax.dot_general(left, right, (((0,), (0,)), ((), ())), precision=HIGHEST, preferred_element_type=jnp.float32)


def eliminate(a_ref, m_ref, first, last):
    size = a_ref.shape[0]
    sub = lax.broadcasted_iota(jnp.int32, (size, 1), 0)
    lane = lax.broadcasted_iota(jnp.int32, (size, size), 1)
    lane_row = lax.broadcasted_iota(jnp.int32, (1, size), 1)

    def step(index, carry):
        j = index * GROUP
        a = a_ref[...]
        rows = [a_ref[pl.ds(j + t, 1), :] for t in range(GROUP)]
        mrows = [m_ref[pl.ds(j + t, 1), :] for t in range(GROUP)]
        cols = [jnp.sum(jnp.where(lane == j + t, a, 0.0), axis=1, keepdims=True) for t in range(GROUP)]
        head = {
            (t, u): jnp.sum(jnp.where(lane_row == j + u, rows[t], 0.0), axis=1, keepdims=True)
            for t in range(GROUP)
            for u in range(t, GROUP)
        }
        m = m_ref[...]
        for t in range(GROUP):
            inverse = 1.0 / head[t, t]
            factor = jnp.where(sub > j + t, cols[t] * inverse, 0.0)
            ratio = {u: head[t, u] * inverse for u in range(t + 1, GROUP)}
            for u in range(t + 1, GROUP):
                cols[u] = cols[u] - factor * head[t, u]
            for u in range(t + 1, GROUP):
                for v in range(u, GROUP):
                    head[u, v] = head[u, v] - ratio[u] * head[t, v]
            for u in range(t + 1, GROUP):
                rows[u] = rows[u] - ratio[u] * rows[t]
                mrows[u] = mrows[u] - ratio[u] * mrows[t]
            a = a - factor * rows[t]
            m = m - factor * mrows[t]
        a_ref[...] = a
        m_ref[...] = m
        return carry

    lax.fori_loop(first // GROUP, last // GROUP, step, 0)


def scale_rows(a_ref, m_ref):
    size = a_ref.shape[0]
    sub = lax.broadcasted_iota(jnp.int32, (size, size), 0)
    lane = lax.broadcasted_iota(jnp.int32, (size, size), 1)
    a = a_ref[...]
    diagonal = jnp.sum(jnp.where(lane == sub, a, 0.0), axis=1, keepdims=True)
    scale = 1.0 / jnp.sqrt(diagonal)
    return jnp.where(lane >= sub, a * scale, 0.0), m_ref[...] * scale


def unit(size):
    sub = lax.broadcasted_iota(jnp.int32, (size, size), 0)
    lane = lax.broadcasted_iota(jnp.int32, (size, size), 1)
    return jnp.where(lane == sub, 1.0, 0.0).astype(jnp.float32)


def factor_kernel(
    nr, nc,
    panel, trailing, block, trail, upper_out, coupling_out, weights_out,
    gram, gram_stage, col_stage, gram_sum, cross, cross_stage, cross_sum, work, minv, inv,
    load_sem, y_send, y_recv, half_send, half_recv, fwd_send, fwd_recv,
    rs_send, rs_recv, cx_send, cx_recv, ag_send, ag_recv, xrs_send, xrs_recv, xag_send, xag_recv,
):
    me_r, me_c = lax.axis_index("rows"), lax.axis_index("cols")
    depth, width = panel.shape
    half = nc // 2
    side, place = me_c // half, lax.rem(me_c, half)
    across = lax.rem(me_c + half, nc)
    chunk = depth // CHUNKS
    piece = width // nr
    groups = cross.shape[0]
    per_group = CHUNKS // groups
    deep = depth // per_group
    wide = width // groups
    cross_piece = wide // nr
    hw = width // 2
    sends = []

    def remote(src, dst, send, recv, where):
        copy = pltpu.make_async_remote_copy(
            src_ref=src, dst_ref=dst, send_sem=send, recv_sem=recv, device_id=where, device_id_type=MESH
        )
        copy.start()
        sends.append(copy)
        return copy

    load_panel = pltpu.make_async_copy(panel, block.at[me_c], load_sem.at[0])
    load_panel.start()
    load_trail = pltpu.make_async_copy(trailing, trail, load_sem.at[1])
    load_trail.start()

    barrier = pltpu.get_barrier_semaphore()
    for d in range(1, nr):
        pl.semaphore_signal(barrier, inc=1, device_id={"rows": lax.rem(me_r + d, nr)}, device_id_type=MESH)
    for d in range(1, nc):
        pl.semaphore_signal(barrier, inc=1, device_id={"cols": lax.rem(me_c + d, nc)}, device_id_type=MESH)
    pl.semaphore_wait(barrier, nr + nc - 2)

    def item(k):
        return pl.ds((k % per_group) * deep, deep), pl.ds((k // per_group) * wide, wide)

    y_copies = []

    def send_across(k):
        rows, lanes = item(k)
        y_copies.append(
            remote(panel.at[rows, lanes], block.at[me_c, rows, lanes], y_send.at[k], y_recv.at[k], {"cols": across})
        )

    for k in range(EARLY):
        send_across(k)
    half_copies = []
    for d in range(1, half):
        peer = side * half + lax.rem(place + d, half)
        half_copies.append(remote(panel, block.at[me_c], half_send.at[d], half_recv.at[d], {"cols": peer}))

    def add_cross(source):
        def step(i, carry):
            rows = pl.ds(pl.multiple_of(i * chunk, chunk), chunk)
            long = pl.ds(pl.multiple_of(source * depth + i * chunk, chunk), chunk)
            product = dot_t(block[source, rows, :], trail[long, :])
            for g in range(groups):
                cross[g] += product[g * wide : (g + 1) * wide, :]
            return carry

        lax.fori_loop(0, CHUNKS, step, 0)

    def add_item(source, k):
        rows, lanes = item(k)
        long = pl.ds(pl.multiple_of(source * depth + (k % per_group) * deep, deep), deep)
        cross[k // per_group] += dot_t(block[source, rows, lanes], trail[long, :])

    load_panel.wait()
    gram[...] = jnp.zeros_like(gram)

    def gram_step(i, carry):
        rows = block[me_c, pl.ds(pl.multiple_of(i * chunk, chunk), chunk), :]
        gram[...] += dot_t(rows, rows)
        return carry

    lax.fori_loop(0, CHUNKS, gram_step, 0)

    def scatter(total, stage, send, recv, piece=piece):
        copies = []
        for d in range(1, nr):
            peer = lax.rem(me_r + d, nr)
            rows = pl.ds(pl.multiple_of(peer * piece, piece), piece)
            copies.append(remote(total.at[rows], stage.at[d], send.at[d], recv.at[d], {"rows": peer}))
        return copies

    def gather(total, send, recv, piece=piece):
        rows = pl.ds(pl.multiple_of(me_r * piece, piece), piece)
        return [
            remote(total.at[rows], total.at[rows], send.at[d], recv.at[d], {"rows": lax.rem(me_r + d, nr)})
            for d in range(1, nr)
        ]

    def arrived(copies):
        for copy in copies:
            copy.wait_recv()

    mine = pl.ds(pl.multiple_of(me_r * piece, piece), piece)
    cross_mine = pl.ds(pl.multiple_of(me_r * cross_piece, cross_piece), cross_piece)

    def summed(total, stage, mine=mine):
        value = total[mine, :]
        for d in range(1, nr):
            value = value + stage[d]
        return value

    gram_rs = scatter(gram, gram_stage, rs_send, rs_recv)
    load_trail.wait()
    cross[...] = jnp.zeros_like(cross)
    add_cross(me_c)
    arrived(gram_rs)
    col_stage[me_c] = summed(gram, gram_stage)
    exchange = [
        remote(col_stage.at[me_c], col_stage.at[me_c], cx_send.at[d], cx_recv.at[d], {"cols": lax.rem(me_c + d, nc)})
        for d in range(1, nc)
    ]
    for k in range(EARLY, CHUNKS):
        send_across(k)
    for d in range(1, half):
        half_copies[d - 1].wait_recv()
        source = side * half + lax.rem(place + half - d, half)
        add_cross(source)
    arrived(exchange)
    value = col_stage[0]
    for c in range(1, nc):
        value = value + col_stage[c]
    gram_sum[mine, :] = value
    gram_ag = gather(gram_sum, ag_send, ag_recv)

    forwards = {}

    def take(k):
        y_copies[k].wait_recv()
        rows, lanes = item(k)
        for d in range(1, half):
            peer = side * half + lax.rem(place + d, half)
            slot = (d - 1) * CHUNKS + k
            part = block.at[across, rows, lanes]
            forwards[d, k] = remote(part, part, fwd_send.at[slot], fwd_recv.at[slot], {"cols": peer})
        add_item(across, k)

    def take_forward(k):
        for d in range(1, half):
            forwards[d, k].wait_recv()
            source = (1 - side) * half + lax.rem(place + half - d, half)
            add_item(source, k)

    cross_rs, cross_ag = {}, {}

    def start_cross(g):
        cross_rs[g] = scatter(cross.at[g], cross_stage.at[g], xrs_send.at[g], xrs_recv.at[g], cross_piece)

    def share_cross(g):
        arrived(cross_rs[g])
        cross_sum[g, cross_mine, :] = summed(cross.at[g], cross_stage.at[g], cross_mine)
        cross_ag[g] = gather(cross_sum.at[g], xag_send.at[g], xag_recv.at[g], cross_piece)

    pending = []
    for k in range(CHUNKS):
        pending.append([functools.partial(take, k)] + ([functools.partial(take_forward, k - 1)] if k % per_group else []))
        if k % per_group == per_group - 1:
            pending[-1].append(functools.partial(take_forward, k))
            pending[-1].append(functools.partial(start_cross, k // per_group))
    for g in range(groups - 1):
        pending[(g + 1) * per_group + 1].append(functools.partial(share_cross, g))

    def advance():
        for task in pending.pop(0):
            task()

    def run(first, last, more):
        eliminate(work, minv, first, last)
        if more:
            advance()

    for _ in range(EARLY):
        advance()
    arrived(gram_ag)
    work[...] = gram_sum[pl.ds(0, hw), pl.ds(0, hw)]
    minv[...] = unit(hw)
    quarter = hw // 4
    for q in range(4):
        run(q * quarter, (q + 1) * quarter, MORE[q])
    upper1, inverse1 = scale_rows(work, minv)
    cross1 = dot(inverse1, gram_sum[pl.ds(0, hw), pl.ds(hw, hw)])
    upper_out[pl.ds(0, hw), pl.ds(0, hw)] = upper1
    upper_out[pl.ds(0, hw), pl.ds(hw, hw)] = cross1
    upper_out[pl.ds(hw, hw), pl.ds(0, hw)] = jnp.zeros_like(upper1)
    work[...] = gram_sum[pl.ds(hw, hw), pl.ds(hw, hw)] - dot_t(cross1, cross1)
    inv[pl.ds(0, hw), pl.ds(0, hw)] = inverse1
    minv[...] = unit(hw)
    for q in range(4):
        run(q * quarter, (q + 1) * quarter, MORE[4 + q])
    upper2, inverse2 = scale_rows(work, minv)
    upper_out[pl.ds(hw, hw), pl.ds(hw, hw)] = upper2
    inverse1 = inv[pl.ds(0, hw), pl.ds(0, hw)]
    corner = -dot(inverse2, dot_t(upper_out[pl.ds(0, hw), pl.ds(hw, hw)], inverse1))
    inv[pl.ds(0, hw), pl.ds(hw, hw)] = jnp.zeros_like(inverse1)
    inv[pl.ds(hw, hw), pl.ds(0, hw)] = corner
    inv[pl.ds(hw, hw), pl.ds(hw, hw)] = inverse2
    while pending:
        advance()
    share_cross(groups - 1)
    for g in range(groups):
        arrived(cross_ag[g])
    inverse = inv[...]
    coupling = dot(inverse, jnp.concatenate([cross_sum[g] for g in range(groups)], axis=0))
    coupling_out[...] = coupling
    weights_out[...] = dot_t(inverse, coupling)
    for copy in sends:
        copy.wait_send()


def update_kernel(
    shrink, block, trailing, upper, coupling, weights, r_factor, r_cross, updated,
    small, w_hi, w_lo, out, small_sem, out_sem,
):
    small[0] = upper[...] * shrink
    small[1] = coupling[...] * shrink
    copies = [
        pltpu.make_async_copy(small.at[0], r_factor, small_sem.at[0]),
        pltpu.make_async_copy(small.at[1], r_cross, small_sem.at[1]),
    ]
    for copy in copies:
        copy.start()
    w = weights[...]
    high = w.astype(jnp.bfloat16)
    w_hi[...] = high
    w_lo[...] = (w - high.astype(jnp.float32)).astype(jnp.bfloat16)
    tile = out.shape[0] // TILES

    def mul(left, right):
        return jnp.dot(left, right, preferred_element_type=jnp.float32)

    def window(i):
        return pl.ds(pl.multiple_of(i * tile, tile), tile)

    def store(i):
        return pltpu.make_async_copy(out.at[window(i)], updated.at[window(i)], out_sem.at[i])

    def step(i, carry):
        rows = window(i)
        p = block[rows, :]
        p_hi = p.astype(jnp.bfloat16)
        p_lo = (p - p_hi.astype(jnp.float32)).astype(jnp.bfloat16)
        product = mul(p_hi, w_hi[...]) + (mul(p_lo, w_hi[...]) + mul(p_hi, w_lo[...]))
        out[rows, :] = trailing[rows, :] - product
        store(i).start()
        return carry

    lax.fori_loop(0, TILES, step, 0)
    for i in range(TILES):
        store(i).wait()
    for copy in copies:
        copy.wait()


def local(nr, nc, panel_cols, trailing):
    depth, width = panel_cols.shape
    rows, cols = trailing.shape
    half = nc // 2
    piece = width // nr
    groups = 2 if width % (2 * 8 * nr) == 0 else 1
    wide = width // groups
    f32 = jnp.float32
    square = jax.ShapeDtypeStruct((width, width), f32)
    tall = jax.ShapeDtypeStruct((width, cols), f32)
    dma = pltpu.SemaphoreType.DMA
    vmem = pl.BlockSpec(memory_space=pltpu.VMEM)
    hbm = pl.BlockSpec(memory_space=pltpu.HBM)
    block, trail, upper, coupling, weights = pl.pallas_call(
        functools.partial(factor_kernel, nr, nc),
        out_shape=(jax.ShapeDtypeStruct((nc, depth, width), f32), jax.ShapeDtypeStruct((rows, cols), f32), square, tall, tall),
        in_specs=[hbm, hbm],
        out_specs=(vmem,) * 5,
        scratch_shapes=[
            pltpu.VMEM((width, width), f32),
            pltpu.VMEM((nr, piece, width), f32),
            pltpu.VMEM((nc, piece, width), f32),
            pltpu.VMEM((width, width), f32),
            pltpu.VMEM((groups, wide, cols), f32),
            pltpu.VMEM((groups, nr, wide // nr, cols), f32),
            pltpu.VMEM((groups, wide, cols), f32),
            pltpu.VMEM((width // 2, width // 2), f32),
            pltpu.VMEM((width // 2, width // 2), f32),
            pltpu.VMEM((width, width), f32),
            dma((2,)),
            dma((CHUNKS,)), dma((CHUNKS,)),
            dma((half,)), dma((half,)),
            dma((CHUNKS * half,)), dma((CHUNKS * half,)),
            dma((nr,)), dma((nr,)),
            dma((nc,)), dma((nc,)),
            dma((nr,)), dma((nr,)),
            dma((groups, nr)), dma((groups, nr)),
            dma((groups, nr)), dma((groups, nr)),
        ],
        compiler_params=pltpu.CompilerParams(
            collective_id=0, has_side_effects=True, vmem_limit_bytes=20 * 1024 * 1024
        ),
        name="factor",
    )(*(pltpu.with_memory_space_constraint(x, pltpu.HBM) for x in (panel_cols, trailing)))

    shrink = 1.0 / math.sqrt(rows * nr)
    r_factor, r_cross, updated = pl.pallas_call(
        functools.partial(update_kernel, shrink),
        out_shape=(square, tall, jax.ShapeDtypeStruct((rows, cols), f32)),
        in_specs=[vmem] * 5,
        out_specs=(hbm,) * 3,
        scratch_shapes=[
            pltpu.VMEM((2, width, cols), f32),
            pltpu.VMEM((width, cols), jnp.bfloat16),
            pltpu.VMEM((width, cols), jnp.bfloat16),
            pltpu.VMEM((rows, cols), f32),
            dma((2,)),
            dma((TILES,)),
        ],
        compiler_params=pltpu.CompilerParams(vmem_limit_bytes=24 * 1024 * 1024),
        name="update",
    )(block.reshape(rows, width), trail, upper, coupling, weights)
    return r_factor, r_cross, updated


def solution(mesh):
    P = jax.sharding.PartitionSpec
    body = functools.partial(local, mesh.shape["rows"], mesh.shape["cols"])
    in_specs = (P(("rows", "cols"), None), P("rows", "cols"))
    out_specs = (P(), P(None, "cols"), P("rows", "cols"))
    return jax.shard_map(body, mesh=mesh, in_specs=in_specs, out_specs=out_specs, check_vma=False)
```

```python
import functools
import math

import jax
import jax.numpy as jnp
from jax import lax
from jax.experimental import pallas as pl
from jax.experimental.pallas import tpu as pltpu

MESH = pl.DeviceIdType.MESH
HIGHEST = lax.Precision.HIGHEST
CHUNKS = 8
ITEMS = 16
EARLY = 6
MORE = (2, 2, 2, 0, 2, 0, 2, 0)
GROUP = 4
TILES = 16


def dot(left, right):
    return lax.dot_general(left, right, (((1,), (0,)), ((), ())), precision=HIGHEST, preferred_element_type=jnp.float32)


def dot_t(left, right):
    return lax.dot_general(left, right, (((0,), (0,)), ((), ())), precision=HIGHEST, preferred_element_type=jnp.float32)


def eliminate(a_ref, m_ref, first, last):
    size = a_ref.shape[0]
    sub = lax.broadcasted_iota(jnp.int32, (size, 1), 0)
    lane = lax.broadcasted_iota(jnp.int32, (size, size), 1)
    lane_row = lax.broadcasted_iota(jnp.int32, (1, size), 1)

    def step(index, carry):
        j = index * GROUP
        a = a_ref[...]
        rows = [a_ref[pl.ds(j + t, 1), :] for t in range(GROUP)]
        mrows = [m_ref[pl.ds(j + t, 1), :] for t in range(GROUP)]
        cols = [jnp.sum(jnp.where(lane == j + t, a, 0.0), axis=1, keepdims=True) for t in range(GROUP)]
        head = {
            (t, u): jnp.sum(jnp.where(lane_row == j + u, rows[t], 0.0), axis=1, keepdims=True)
            for t in range(GROUP)
            for u in range(t, GROUP)
        }
        m = m_ref[...]
        for t in range(GROUP):
            inverse = 1.0 / head[t, t]
            factor = jnp.where(sub > j + t, cols[t] * inverse, 0.0)
            ratio = {u: head[t, u] * inverse for u in range(t + 1, GROUP)}
            for u in range(t + 1, GROUP):
                cols[u] = cols[u] - factor * head[t, u]
            for u in range(t + 1, GROUP):
                for v in range(u, GROUP):
                    head[u, v] = head[u, v] - ratio[u] * head[t, v]
            for u in range(t + 1, GROUP):
                rows[u] = rows[u] - ratio[u] * rows[t]
                mrows[u] = mrows[u] - ratio[u] * mrows[t]
            a = a - factor * rows[t]
            m = m - factor * mrows[t]
        a_ref[...] = a
        m_ref[...] = m
        return carry

    lax.fori_loop(first // GROUP, last // GROUP, step, 0)


def scale_rows(a_ref, m_ref):
    size = a_ref.shape[0]
    sub = lax.broadcasted_iota(jnp.int32, (size, size), 0)
    lane = lax.broadcasted_iota(jnp.int32, (size, size), 1)
    a = a_ref[...]
    diagonal = jnp.sum(jnp.where(lane == sub, a, 0.0), axis=1, keepdims=True)
    scale = 1.0 / jnp.sqrt(diagonal)
    return jnp.where(lane >= sub, a * scale, 0.0), m_ref[...] * scale


def unit(size):
    sub = lax.broadcasted_iota(jnp.int32, (size, size), 0)
    lane = lax.broadcasted_iota(jnp.int32, (size, size), 1)
    return jnp.where(lane == sub, 1.0, 0.0).astype(jnp.float32)


def factor_kernel(
    nr, nc,
    panel, trailing, block, trail, upper_out, coupling_out, weights_out,
    gram, gram_stage, col_stage, gram_sum, cross, cross_stage, cross_sum, work, minv, inv, square,
    load_sem, y_send, y_recv, half_send, half_recv, fwd_send, fwd_recv,
    rs_send, rs_recv, cx_send, cx_recv, ag_send, ag_recv, xrs_send, xrs_recv, xag_send, xag_recv,
):
    me_r, me_c = lax.axis_index("rows"), lax.axis_index("cols")
    depth, width = panel.shape
    half = nc // 2
    side, place = me_c // half, lax.rem(me_c, half)
    across = lax.rem(me_c + half, nc)
    chunk = depth // CHUNKS
    piece = width // nr
    groups = cross.shape[0]
    per_group = ITEMS // groups
    deep = depth // per_group
    wide = width // groups
    cross_piece = wide // nr
    hw = width // 2
    sends = []

    def remote(src, dst, send, recv, where):
        copy = pltpu.make_async_remote_copy(
            src_ref=src, dst_ref=dst, send_sem=send, recv_sem=recv, device_id=where, device_id_type=MESH
        )
        copy.start()
        sends.append(copy)
        return copy

    load_panel = pltpu.make_async_copy(panel, block.at[me_c], load_sem.at[0])
    load_panel.start()
    load_trail = pltpu.make_async_copy(trailing, trail, load_sem.at[1])
    load_trail.start()

    barrier = pltpu.get_barrier_semaphore()
    for d in range(1, nr):
        pl.semaphore_signal(barrier, inc=1, device_id={"rows": lax.rem(me_r + d, nr)}, device_id_type=MESH)
    for d in range(1, nc):
        pl.semaphore_signal(barrier, inc=1, device_id={"cols": lax.rem(me_c + d, nc)}, device_id_type=MESH)
    pl.semaphore_wait(barrier, nr + nc - 2)

    def item(k):
        return pl.ds((k % per_group) * deep, deep), pl.ds((k // per_group) * wide, wide)

    y_copies = []

    def send_across(k):
        rows, lanes = item(k)
        y_copies.append(
            remote(panel.at[rows, lanes], block.at[me_c, rows, lanes], y_send.at[k], y_recv.at[k], {"cols": across})
        )

    for k in range(EARLY):
        send_across(k)
    half_copies = []
    for d in range(1, half):
        peer = side * half + lax.rem(place + d, half)
        half_copies.append(remote(panel, block.at[me_c], half_send.at[d], half_recv.at[d], {"cols": peer}))

    def add_cross(source):
        def step(i, carry):
            rows = pl.ds(pl.multiple_of(i * chunk, chunk), chunk)
            long = pl.ds(pl.multiple_of(source * depth + i * chunk, chunk), chunk)
            product = dot_t(block[source, rows, :], trail[long, :])
            for g in range(groups):
                cross[g] += product[g * wide : (g + 1) * wide, :]
            return carry

        lax.fori_loop(0, CHUNKS, step, 0)

    def add_item(source, k):
        rows, lanes = item(k)
        long = pl.ds(pl.multiple_of(source * depth + (k % per_group) * deep, deep), deep)
        cross[k // per_group] += dot_t(block[source, rows, lanes], trail[long, :])

    load_panel.wait()
    gram[...] = jnp.zeros_like(gram)

    def gram_step(i, carry):
        rows = block[me_c, pl.ds(pl.multiple_of(i * chunk, chunk), chunk), :]
        gram[...] += dot_t(rows, rows)
        return carry

    lax.fori_loop(0, CHUNKS, gram_step, 0)

    def scatter(total, stage, send, recv, piece=piece):
        copies = []
        for d in range(1, nr):
            peer = lax.rem(me_r + d, nr)
            rows = pl.ds(pl.multiple_of(peer * piece, piece), piece)
            copies.append(remote(total.at[rows], stage.at[d], send.at[d], recv.at[d], {"rows": peer}))
        return copies

    def gather(total, send, recv, piece=piece):
        rows = pl.ds(pl.multiple_of(me_r * piece, piece), piece)
        return [
            remote(total.at[rows], total.at[rows], send.at[d], recv.at[d], {"rows": lax.rem(me_r + d, nr)})
            for d in range(1, nr)
        ]

    def arrived(copies):
        for copy in copies:
            copy.wait_recv()

    mine = pl.ds(pl.multiple_of(me_r * piece, piece), piece)
    cross_mine = pl.ds(pl.multiple_of(me_r * cross_piece, cross_piece), cross_piece)

    def summed(total, stage, mine=mine):
        value = total[mine, :]
        for d in range(1, nr):
            value = value + stage[d]
        return value

    gram_rs = scatter(gram, gram_stage, rs_send, rs_recv)
    load_trail.wait()
    cross[...] = jnp.zeros_like(cross)
    add_cross(me_c)
    arrived(gram_rs)
    col_stage[me_c] = summed(gram, gram_stage)
    exchange = [
        remote(col_stage.at[me_c], col_stage.at[me_c], cx_send.at[d], cx_recv.at[d], {"cols": lax.rem(me_c + d, nc)})
        for d in range(1, nc)
    ]
    for k in range(EARLY, ITEMS):
        send_across(k)
    for d in range(1, half):
        half_copies[d - 1].wait_recv()
        source = side * half + lax.rem(place + half - d, half)
        add_cross(source)
    arrived(exchange)
    value = col_stage[0]
    for c in range(1, nc):
        value = value + col_stage[c]
    gram_sum[mine, :] = value
    gram_ag = gather(gram_sum, ag_send, ag_recv)

    forwards = {}

    def take(k):
        y_copies[k].wait_recv()
        rows, lanes = item(k)
        for d in range(1, half):
            peer = side * half + lax.rem(place + d, half)
            slot = (d - 1) * ITEMS + k
            part = block.at[across, rows, lanes]
            forwards[d, k] = remote(part, part, fwd_send.at[slot], fwd_recv.at[slot], {"cols": peer})
        add_item(across, k)

    def take_forward(k):
        for d in range(1, half):
            forwards[d, k].wait_recv()
            source = (1 - side) * half + lax.rem(place + half - d, half)
            add_item(source, k)

    cross_rs, cross_ag = {}, {}

    def start_cross(g):
        cross_rs[g] = scatter(cross.at[g], cross_stage.at[g], xrs_send.at[g], xrs_recv.at[g], cross_piece)

    def share_cross(g):
        arrived(cross_rs[g])
        cross_sum[g, cross_mine, :] = summed(cross.at[g], cross_stage.at[g], cross_mine)
        cross_ag[g] = gather(cross_sum.at[g], xag_send.at[g], xag_recv.at[g], cross_piece)

    pending = []
    for k in range(ITEMS):
        pending.append(([functools.partial(take_forward, k - 1)] if k % per_group else []) + [functools.partial(take, k)])
        if k % per_group == per_group - 1:
            pending[-1].append(functools.partial(take_forward, k))
            pending[-1].append(functools.partial(start_cross, k // per_group))
    for g in range(groups - 1):
        pending[(g + 1) * per_group + 2].append(functools.partial(share_cross, g))

    def advance():
        for task in pending.pop(0):
            task()

    def run(first, last, more):
        eliminate(work, minv, first, last)
        for _ in range(more):
            advance()

    for _ in range(EARLY):
        advance()
    arrived(gram_ag)
    work[...] = gram_sum[pl.ds(0, hw), pl.ds(0, hw)]
    minv[...] = unit(hw)
    quarter = hw // 4
    for q in range(4):
        run(q * quarter, (q + 1) * quarter, MORE[q])
    upper1, inverse1 = scale_rows(work, minv)
    cross1 = dot(inverse1, gram_sum[pl.ds(0, hw), pl.ds(hw, hw)])
    upper_out[pl.ds(0, hw), pl.ds(0, hw)] = upper1
    upper_out[pl.ds(0, hw), pl.ds(hw, hw)] = cross1
    upper_out[pl.ds(hw, hw), pl.ds(0, hw)] = jnp.zeros_like(upper1)
    work[...] = gram_sum[pl.ds(hw, hw), pl.ds(hw, hw)] - dot_t(cross1, cross1)
    inv[pl.ds(0, hw), pl.ds(0, hw)] = inverse1
    minv[...] = unit(hw)
    for q in range(4):
        run(q * quarter, (q + 1) * quarter, MORE[4 + q])
    upper2, inverse2 = scale_rows(work, minv)
    upper_out[pl.ds(hw, hw), pl.ds(hw, hw)] = upper2
    inverse1 = inv[pl.ds(0, hw), pl.ds(0, hw)]
    corner = -dot(inverse2, dot_t(upper_out[pl.ds(0, hw), pl.ds(hw, hw)], inverse1))
    inv[pl.ds(0, hw), pl.ds(hw, hw)] = jnp.zeros_like(inverse1)
    inv[pl.ds(hw, hw), pl.ds(0, hw)] = corner
    inv[pl.ds(hw, hw), pl.ds(hw, hw)] = inverse2
    while pending:
        advance()
    inverse = inv[...]
    square[...] = dot_t(inverse, inverse)
    last = slice((groups - 1) * wide, groups * wide)
    coupling_out[...] = jnp.zeros_like(coupling_out)
    weights_out[...] = jnp.zeros_like(weights_out)
    for g in range(groups - 1):
        arrived(cross_ag[g])
        part = cross_sum[g]
        coupling_out[...] += dot(inv[:, g * wide : (g + 1) * wide], part)
        weights_out[...] += dot(square[:, g * wide : (g + 1) * wide], part)
    share_cross(groups - 1)
    arrived(cross_ag[groups - 1])
    part = cross_sum[groups - 1]
    weights_out[...] += dot(square[:, last], part)
    coupling_out[...] += dot(inv[:, last], part)
    for copy in sends:
        copy.wait_send()


def update_kernel(
    shrink, block, trailing, upper, coupling, weights, r_factor, r_cross, updated,
    small, w_hi, w_lo, out, small_sem, out_sem,
):
    small[0] = upper[...] * shrink
    small[1] = coupling[...] * shrink
    copies = [
        pltpu.make_async_copy(small.at[0], r_factor, small_sem.at[0]),
        pltpu.make_async_copy(small.at[1], r_cross, small_sem.at[1]),
    ]
    for copy in copies:
        copy.start()
    w = weights[...]
    high = w.astype(jnp.bfloat16)
    w_hi[...] = high
    w_lo[...] = (w - high.astype(jnp.float32)).astype(jnp.bfloat16)
    tile = out.shape[0] // TILES

    def mul(left, right):
        return jnp.dot(left, right, preferred_element_type=jnp.float32)

    def window(i):
        return pl.ds(pl.multiple_of(i * tile, tile), tile)

    def store(i):
        return pltpu.make_async_copy(out.at[window(i)], updated.at[window(i)], out_sem.at[i])

    def step(i, carry):
        rows = window(i)
        p = block[rows, :]
        p_hi = p.astype(jnp.bfloat16)
        p_lo = (p - p_hi.astype(jnp.float32)).astype(jnp.bfloat16)
        product = mul(p_hi, w_hi[...]) + (mul(p_lo, w_hi[...]) + mul(p_hi, w_lo[...]))
        out[rows, :] = trailing[rows, :] - product
        store(i).start()
        return carry

    lax.fori_loop(0, TILES, step, 0)
    for i in range(TILES):
        store(i).wait()
    for copy in copies:
        copy.wait()


def local(nr, nc, panel_cols, trailing):
    depth, width = panel_cols.shape
    rows, cols = trailing.shape
    half = nc // 2
    piece = width // nr
    groups = 2 if width % (2 * 8 * nr) == 0 else 1
    wide = width // groups
    f32 = jnp.float32
    square = jax.ShapeDtypeStruct((width, width), f32)
    tall = jax.ShapeDtypeStruct((width, cols), f32)
    dma = pltpu.SemaphoreType.DMA
    vmem = pl.BlockSpec(memory_space=pltpu.VMEM)
    hbm = pl.BlockSpec(memory_space=pltpu.HBM)
    block, trail, upper, coupling, weights = pl.pallas_call(
        functools.partial(factor_kernel, nr, nc),
        out_shape=(jax.ShapeDtypeStruct((nc, depth, width), f32), jax.ShapeDtypeStruct((rows, cols), f32), square, tall, tall),
        in_specs=[hbm, hbm],
        out_specs=(vmem,) * 5,
        scratch_shapes=[
            pltpu.VMEM((width, width), f32),
            pltpu.VMEM((nr, piece, width), f32),
            pltpu.VMEM((nc, piece, width), f32),
            pltpu.VMEM((width, width), f32),
            pltpu.VMEM((groups, wide, cols), f32),
            pltpu.VMEM((groups, nr, wide // nr, cols), f32),
            pltpu.VMEM((groups, wide, cols), f32),
            pltpu.VMEM((width // 2, width // 2), f32),
            pltpu.VMEM((width // 2, width // 2), f32),
            pltpu.VMEM((width, width), f32),
            pltpu.VMEM((width, width), f32),
            dma((2,)),
            dma((ITEMS,)), dma((ITEMS,)),
            dma((half,)), dma((half,)),
            dma((ITEMS * half,)), dma((ITEMS * half,)),
            dma((nr,)), dma((nr,)),
            dma((nc,)), dma((nc,)),
            dma((nr,)), dma((nr,)),
            dma((groups, nr)), dma((groups, nr)),
            dma((groups, nr)), dma((groups, nr)),
        ],
        compiler_params=pltpu.CompilerParams(
            collective_id=0, has_side_effects=True, vmem_limit_bytes=20 * 1024 * 1024
        ),
        name="factor",
    )(*(pltpu.with_memory_space_constraint(x, pltpu.HBM) for x in (panel_cols, trailing)))

    shrink = 1.0 / math.sqrt(rows * nr)
    r_factor, r_cross, updated = pl.pallas_call(
        functools.partial(update_kernel, shrink),
        out_shape=(square, tall, jax.ShapeDtypeStruct((rows, cols), f32)),
        in_specs=[vmem] * 5,
        out_specs=(hbm,) * 3,
        scratch_shapes=[
            pltpu.VMEM((2, width, cols), f32),
            pltpu.VMEM((width, cols), jnp.bfloat16),
            pltpu.VMEM((width, cols), jnp.bfloat16),
            pltpu.VMEM((rows, cols), f32),
            dma((2,)),
            dma((TILES,)),
        ],
        compiler_params=pltpu.CompilerParams(vmem_limit_bytes=24 * 1024 * 1024),
        name="update",
    )(block.reshape(rows, width), trail, upper, coupling, weights)
    return r_factor, r_cross, updated


def solution(mesh):
    P = jax.sharding.PartitionSpec
    body = functools.partial(local, mesh.shape["rows"], mesh.shape["cols"])
    in_specs = (P(("rows", "cols"), None), P("rows", "cols"))
    out_specs = (P(), P(None, "cols"), P("rows", "cols"))
    return jax.shard_map(body, mesh=mesh, in_specs=in_specs, out_specs=out_specs, check_vma=False)
```

```python
import functools
import math

import jax
import jax.numpy as jnp
from jax import lax
from jax.experimental import pallas as pl
from jax.experimental.pallas import tpu as pltpu

MESH = pl.DeviceIdType.MESH
HIGHEST = lax.Precision.HIGHEST
CHUNKS = 8
ITEMS = 8
EARLY = 3
MORE = (1, 1, 1, 0, 1, 0, 1, 0)
GROUP = 4
TILES = 8


def dot(left, right):
    return lax.dot_general(left, right, (((1,), (0,)), ((), ())), precision=HIGHEST, preferred_element_type=jnp.float32)


def dot_t(left, right):
    return lax.dot_general(left, right, (((0,), (0,)), ((), ())), precision=HIGHEST, preferred_element_type=jnp.float32)


def eliminate(a_ref, m_ref, first, last):
    size = a_ref.shape[0]
    sub = lax.broadcasted_iota(jnp.int32, (size, 1), 0)
    lane = lax.broadcasted_iota(jnp.int32, (size, size), 1)
    lane_row = lax.broadcasted_iota(jnp.int32, (1, size), 1)

    def step(index, carry):
        j = index * GROUP
        a = a_ref[...]
        rows = [a_ref[pl.ds(j + t, 1), :] for t in range(GROUP)]
        mrows = [m_ref[pl.ds(j + t, 1), :] for t in range(GROUP)]
        cols = [jnp.sum(jnp.where(lane == j + t, a, 0.0), axis=1, keepdims=True) for t in range(GROUP)]
        head = {
            (t, u): jnp.sum(jnp.where(lane_row == j + u, rows[t], 0.0), axis=1, keepdims=True)
            for t in range(GROUP)
            for u in range(t, GROUP)
        }
        m = m_ref[...]
        for t in range(GROUP):
            inverse = 1.0 / head[t, t]
            factor = jnp.where(sub > j + t, cols[t] * inverse, 0.0)
            ratio = {u: head[t, u] * inverse for u in range(t + 1, GROUP)}
            for u in range(t + 1, GROUP):
                cols[u] = cols[u] - factor * head[t, u]
            for u in range(t + 1, GROUP):
                for v in range(u, GROUP):
                    head[u, v] = head[u, v] - ratio[u] * head[t, v]
            for u in range(t + 1, GROUP):
                rows[u] = rows[u] - ratio[u] * rows[t]
                mrows[u] = mrows[u] - ratio[u] * mrows[t]
            a = a - factor * rows[t]
            m = m - factor * mrows[t]
        a_ref[...] = a
        m_ref[...] = m
        return carry

    lax.fori_loop(first // GROUP, last // GROUP, step, 0)


def scale_rows(a_ref, m_ref):
    size = a_ref.shape[0]
    sub = lax.broadcasted_iota(jnp.int32, (size, size), 0)
    lane = lax.broadcasted_iota(jnp.int32, (size, size), 1)
    a = a_ref[...]
    diagonal = jnp.sum(jnp.where(lane == sub, a, 0.0), axis=1, keepdims=True)
    scale = 1.0 / jnp.sqrt(diagonal)
    return jnp.where(lane >= sub, a * scale, 0.0), m_ref[...] * scale


def unit(size):
    sub = lax.broadcasted_iota(jnp.int32, (size, size), 0)
    lane = lax.broadcasted_iota(jnp.int32, (size, size), 1)
    return jnp.where(lane == sub, 1.0, 0.0).astype(jnp.float32)


def factor_kernel(
    nr, nc,
    panel, trailing, block, trail, upper_out, coupling_out, weights_out,
    gram, gram_stage, col_stage, gram_sum, cross, cross_stage, cross_sum, work, minv, inv, square,
    load_sem, y_send, y_recv, half_send, half_recv, fwd_send, fwd_recv,
    rs_send, rs_recv, cx_send, cx_recv, ag_send, ag_recv, xrs_send, xrs_recv, xag_send, xag_recv,
):
    me_r, me_c = lax.axis_index("rows"), lax.axis_index("cols")
    depth, width = panel.shape
    half = nc // 2
    side, place = me_c // half, lax.rem(me_c, half)
    across = lax.rem(me_c + half, nc)
    chunk = depth // CHUNKS
    piece = width // nr
    groups = cross.shape[0]
    per_group = ITEMS // groups
    deep = depth // per_group
    wide = width // groups
    cross_piece = wide // nr
    hw = width // 2
    sends = []

    def remote(src, dst, send, recv, where):
        copy = pltpu.make_async_remote_copy(
            src_ref=src, dst_ref=dst, send_sem=send, recv_sem=recv, device_id=where, device_id_type=MESH
        )
        copy.start()
        sends.append(copy)
        return copy

    load_panel = pltpu.make_async_copy(panel, block.at[me_c], load_sem.at[0])
    load_panel.start()
    load_trail = pltpu.make_async_copy(trailing, trail, load_sem.at[1])
    load_trail.start()

    barrier = pltpu.get_barrier_semaphore()
    for d in range(1, nr):
        pl.semaphore_signal(barrier, inc=1, device_id={"rows": lax.rem(me_r + d, nr)}, device_id_type=MESH)
    for d in range(1, nc):
        pl.semaphore_signal(barrier, inc=1, device_id={"cols": lax.rem(me_c + d, nc)}, device_id_type=MESH)
    pl.semaphore_wait(barrier, nr + nc - 2)

    def item(k):
        return pl.ds((k % per_group) * deep, deep), pl.ds((k // per_group) * wide, wide)

    y_copies = []

    def send_across(k):
        rows, lanes = item(k)
        y_copies.append(
            remote(panel.at[rows, lanes], block.at[me_c, rows, lanes], y_send.at[k], y_recv.at[k], {"cols": across})
        )

    for k in range(EARLY):
        send_across(k)
    half_copies = []
    for d in range(1, half):
        peer = side * half + lax.rem(place + d, half)
        half_copies.append(remote(panel, block.at[me_c], half_send.at[d], half_recv.at[d], {"cols": peer}))

    def add_cross(source):
        def step(i, carry):
            rows = pl.ds(pl.multiple_of(i * chunk, chunk), chunk)
            long = pl.ds(pl.multiple_of(source * depth + i * chunk, chunk), chunk)
            product = dot_t(block[source, rows, :], trail[long, :])
            for g in range(groups):
                cross[g] += product[g * wide : (g + 1) * wide, :]
            return carry

        lax.fori_loop(0, CHUNKS, step, 0)

    def add_item(source, k):
        rows, lanes = item(k)
        long = pl.ds(pl.multiple_of(source * depth + (k % per_group) * deep, deep), deep)
        cross[k // per_group] += dot_t(block[source, rows, lanes], trail[long, :])

    load_panel.wait()
    gram[...] = jnp.zeros_like(gram)

    def gram_step(i, carry):
        rows = block[me_c, pl.ds(pl.multiple_of(i * chunk, chunk), chunk), :]
        gram[...] += dot_t(rows, rows)
        return carry

    lax.fori_loop(0, CHUNKS, gram_step, 0)

    def scatter(total, stage, send, recv, piece=piece):
        copies = []
        for d in range(1, nr):
            peer = lax.rem(me_r + d, nr)
            rows = pl.ds(pl.multiple_of(peer * piece, piece), piece)
            copies.append(remote(total.at[rows], stage.at[d], send.at[d], recv.at[d], {"rows": peer}))
        return copies

    def gather(total, send, recv, piece=piece):
        rows = pl.ds(pl.multiple_of(me_r * piece, piece), piece)
        return [
            remote(total.at[rows], total.at[rows], send.at[d], recv.at[d], {"rows": lax.rem(me_r + d, nr)})
            for d in range(1, nr)
        ]

    def arrived(copies):
        for copy in copies:
            copy.wait_recv()

    mine = pl.ds(pl.multiple_of(me_r * piece, piece), piece)
    cross_mine = pl.ds(pl.multiple_of(me_r * cross_piece, cross_piece), cross_piece)

    def summed(total, stage, mine=mine):
        value = total[mine, :]
        for d in range(1, nr):
            value = value + stage[d]
        return value

    gram_rs = scatter(gram, gram_stage, rs_send, rs_recv)
    load_trail.wait()
    cross[...] = jnp.zeros_like(cross)
    add_cross(me_c)
    arrived(gram_rs)
    col_stage[me_c] = summed(gram, gram_stage)
    exchange = [
        remote(col_stage.at[me_c], col_stage.at[me_c], cx_send.at[d], cx_recv.at[d], {"cols": lax.rem(me_c + d, nc)})
        for d in range(1, nc)
    ]
    for k in range(EARLY, ITEMS):
        send_across(k)
    for d in range(1, half):
        half_copies[d - 1].wait_recv()
        source = side * half + lax.rem(place + half - d, half)
        add_cross(source)
    arrived(exchange)
    value = col_stage[0]
    for c in range(1, nc):
        value = value + col_stage[c]
    gram_sum[mine, :] = value
    gram_ag = gather(gram_sum, ag_send, ag_recv)

    forwards = {}

    def take(k):
        y_copies[k].wait_recv()
        rows, lanes = item(k)
        for d in range(1, half):
            peer = side * half + lax.rem(place + d, half)
            slot = (d - 1) * ITEMS + k
            part = block.at[across, rows, lanes]
            forwards[d, k] = remote(part, part, fwd_send.at[slot], fwd_recv.at[slot], {"cols": peer})
        add_item(across, k)

    def take_forward(k):
        for d in range(1, half):
            forwards[d, k].wait_recv()
            source = (1 - side) * half + lax.rem(place + half - d, half)
            add_item(source, k)

    cross_rs, cross_ag = {}, {}

    def start_cross(g):
        cross_rs[g] = scatter(cross.at[g], cross_stage.at[g], xrs_send.at[g], xrs_recv.at[g], cross_piece)

    def share_cross(g):
        arrived(cross_rs[g])
        cross_sum[g, cross_mine, :] = summed(cross.at[g], cross_stage.at[g], cross_mine)
        cross_ag[g] = gather(cross_sum.at[g], xag_send.at[g], xag_recv.at[g], cross_piece)

    pending = []
    for k in range(ITEMS):
        pending.append(([functools.partial(take_forward, k - 1)] if k % per_group else []) + [functools.partial(take, k)])
        if k % per_group == per_group - 1:
            pending[-1].append(functools.partial(take_forward, k))
            pending[-1].append(functools.partial(start_cross, k // per_group))
    for g in range(groups - 1):
        pending[(g + 1) * per_group + 2].append(functools.partial(share_cross, g))

    def advance():
        for task in pending.pop(0):
            task()

    def run(first, last, more):
        eliminate(work, minv, first, last)
        for _ in range(more):
            advance()

    for _ in range(EARLY):
        advance()
    arrived(gram_ag)
    work[...] = gram_sum[pl.ds(0, hw), pl.ds(0, hw)]
    minv[...] = unit(hw)
    quarter = hw // 4
    for q in range(4):
        run(q * quarter, (q + 1) * quarter, MORE[q])
    upper1, inverse1 = scale_rows(work, minv)
    cross1 = dot(inverse1, gram_sum[pl.ds(0, hw), pl.ds(hw, hw)])
    upper_out[pl.ds(0, hw), pl.ds(0, hw)] = upper1
    upper_out[pl.ds(0, hw), pl.ds(hw, hw)] = cross1
    upper_out[pl.ds(hw, hw), pl.ds(0, hw)] = jnp.zeros_like(upper1)
    work[...] = gram_sum[pl.ds(hw, hw), pl.ds(hw, hw)] - dot_t(cross1, cross1)
    inv[pl.ds(0, hw), pl.ds(0, hw)] = inverse1
    minv[...] = unit(hw)
    for q in range(4):
        run(q * quarter, (q + 1) * quarter, MORE[4 + q])
    upper2, inverse2 = scale_rows(work, minv)
    upper_out[pl.ds(hw, hw), pl.ds(hw, hw)] = upper2
    inverse1 = inv[pl.ds(0, hw), pl.ds(0, hw)]
    corner = -dot(inverse2, dot_t(upper_out[pl.ds(0, hw), pl.ds(hw, hw)], inverse1))
    inv[pl.ds(0, hw), pl.ds(hw, hw)] = jnp.zeros_like(inverse1)
    inv[pl.ds(hw, hw), pl.ds(0, hw)] = corner
    inv[pl.ds(hw, hw), pl.ds(hw, hw)] = inverse2
    while pending:
        advance()
    inverse = inv[...]
    square[...] = dot_t(inverse, inverse)
    last = slice((groups - 1) * wide, groups * wide)
    coupling_out[...] = jnp.zeros_like(coupling_out)
    weights_out[...] = jnp.zeros_like(weights_out)
    for g in range(groups - 1):
        arrived(cross_ag[g])
        part = cross_sum[g]
        coupling_out[...] += dot(inv[:, g * wide : (g + 1) * wide], part)
        weights_out[...] += dot(square[:, g * wide : (g + 1) * wide], part)
    share_cross(groups - 1)
    arrived(cross_ag[groups - 1])
    part = cross_sum[groups - 1]
    weights_out[...] += dot(square[:, last], part)
    coupling_out[...] += dot(inv[:, last], part)
    for copy in sends:
        copy.wait_send()


def update_kernel(
    shrink, block, trailing, upper, coupling, weights, r_factor, r_cross, updated,
    small, w_hi, w_lo, out, small_sem, out_sem,
):
    small[0] = upper[...] * shrink
    small[1] = coupling[...] * shrink
    copies = [
        pltpu.make_async_copy(small.at[0], r_factor, small_sem.at[0]),
        pltpu.make_async_copy(small.at[1], r_cross, small_sem.at[1]),
    ]
    for copy in copies:
        copy.start()
    w = weights[...]
    high = w.astype(jnp.bfloat16)
    w_hi[...] = high
    w_lo[...] = (w - high.astype(jnp.float32)).astype(jnp.bfloat16)
    tile = out.shape[0] // TILES

    def mul(left, right):
        return jnp.dot(left, right, preferred_element_type=jnp.float32)

    def window(i):
        return pl.ds(pl.multiple_of(i * tile, tile), tile)

    def store(i):
        return pltpu.make_async_copy(out.at[window(i)], updated.at[window(i)], out_sem.at[i])

    def step(i, carry):
        rows = window(i)
        p = block[rows, :]
        p_hi = p.astype(jnp.bfloat16)
        p_lo = (p - p_hi.astype(jnp.float32)).astype(jnp.bfloat16)
        product = mul(p_hi, w_hi[...]) + (mul(p_lo, w_hi[...]) + mul(p_hi, w_lo[...]))
        out[rows, :] = trailing[rows, :] - product
        store(i).start()
        return carry

    lax.fori_loop(0, TILES, step, 0)
    for i in range(TILES):
        store(i).wait()
    for copy in copies:
        copy.wait()


def local(nr, nc, panel_cols, trailing):
    depth, width = panel_cols.shape
    rows, cols = trailing.shape
    half = nc // 2
    piece = width // nr
    groups = 2 if width % (2 * 8 * nr) == 0 else 1
    wide = width // groups
    f32 = jnp.float32
    square = jax.ShapeDtypeStruct((width, width), f32)
    tall = jax.ShapeDtypeStruct((width, cols), f32)
    dma = pltpu.SemaphoreType.DMA
    vmem = pl.BlockSpec(memory_space=pltpu.VMEM)
    hbm = pl.BlockSpec(memory_space=pltpu.HBM)
    block, trail, upper, coupling, weights = pl.pallas_call(
        functools.partial(factor_kernel, nr, nc),
        out_shape=(jax.ShapeDtypeStruct((nc, depth, width), f32), jax.ShapeDtypeStruct((rows, cols), f32), square, tall, tall),
        in_specs=[hbm, hbm],
        out_specs=(vmem,) * 5,
        scratch_shapes=[
            pltpu.VMEM((width, width), f32),
            pltpu.VMEM((nr, piece, width), f32),
            pltpu.VMEM((nc, piece, width), f32),
            pltpu.VMEM((width, width), f32),
            pltpu.VMEM((groups, wide, cols), f32),
            pltpu.VMEM((groups, nr, wide // nr, cols), f32),
            pltpu.VMEM((groups, wide, cols), f32),
            pltpu.VMEM((width // 2, width // 2), f32),
            pltpu.VMEM((width // 2, width // 2), f32),
            pltpu.VMEM((width, width), f32),
            pltpu.VMEM((width, width), f32),
            dma((2,)),
            dma((ITEMS,)), dma((ITEMS,)),
            dma((half,)), dma((half,)),
            dma((ITEMS * half,)), dma((ITEMS * half,)),
            dma((nr,)), dma((nr,)),
            dma((nc,)), dma((nc,)),
            dma((nr,)), dma((nr,)),
            dma((groups, nr)), dma((groups, nr)),
            dma((groups, nr)), dma((groups, nr)),
        ],
        compiler_params=pltpu.CompilerParams(
            collective_id=0, has_side_effects=True, vmem_limit_bytes=20 * 1024 * 1024
        ),
        name="factor",
    )(*(pltpu.with_memory_space_constraint(x, pltpu.HBM) for x in (panel_cols, trailing)))

    shrink = 1.0 / math.sqrt(rows * nr)
    r_factor, r_cross, updated = pl.pallas_call(
        functools.partial(update_kernel, shrink),
        out_shape=(square, tall, jax.ShapeDtypeStruct((rows, cols), f32)),
        in_specs=[vmem] * 5,
        out_specs=(hbm,) * 3,
        scratch_shapes=[
            pltpu.VMEM((2, width, cols), f32),
            pltpu.VMEM((width, cols), jnp.bfloat16),
            pltpu.VMEM((width, cols), jnp.bfloat16),
            pltpu.VMEM((rows, cols), f32),
            dma((2,)),
            dma((TILES,)),
        ],
        compiler_params=pltpu.CompilerParams(vmem_limit_bytes=24 * 1024 * 1024),
        name="update",
    )(block.reshape(rows, width), trail, upper, coupling, weights)
    return r_factor, r_cross, updated


def solution(mesh):
    P = jax.sharding.PartitionSpec
    body = functools.partial(local, mesh.shape["rows"], mesh.shape["cols"])
    in_specs = (P(("rows", "cols"), None), P("rows", "cols"))
    out_specs = (P(), P(None, "cols"), P("rows", "cols"))
    return jax.shard_map(body, mesh=mesh, in_specs=in_specs, out_specs=out_specs, check_vma=False)
```
